32 devices in a mesh: blk: 8 (over y, x, core), walk: 4 (over z).
Axes of the slice: x: 2, y: 2, z: 4, core: 2. Of those that a mesh axis runs over, the one named last changes fastest.
Arguments:
- walkers: bfloat16 [64, 200, 2048], P(('blk', 'walk')), may hold values from -6 to 6
- inv_intersection: bfloat16 [64, 2, 100, 100], P(('blk', 'walk')), may hold values from -0.625 to 0.625
- rotated_chol: bfloat16 [16, 100, 2048], P('blk'), may hold values from -0.013671875 to 0.013671875
- full_chol: bfloat16 [16, 2048, 2048], P('walk', 'blk'), may hold values from -0.125 to 0.125
- field_noise: float32 [16], replicated, may hold values from -4 to 4
Outputs:
- propagated: bfloat16 [64, 200, 2048], P(('blk', 'walk'))
- force_bias: float32 [64, 16], P(('blk', 'walk'))
- bias_shift: float32 [16], replicated
The draws below stay inside these ranges and needn't reach their ends.
All inputs are finite; a program needn't handle non-finite values.
Results may differ from the reference program's by a relative error of at most 0.0065.
Values may be sent and summed in bfloat16 or wider, within the bound.
A program may use at most 128 MiB of HBM per device.

```python
import jax
import jax.numpy as jnp
from jax import lax

NORB = 2048
NOCC = 100
WALKERS = 64
CHOL = 16


def block_levels(stream_key, shape, split, least, top_value):
    loudness = 1.0
    for position, parts in split:
        draws = jax.random.uniform(jax.random.fold_in(jax.random.fold_in(stream_key, 6), position), (parts,), jnp.float32, least / len(split), top_value / len(split))
        loudness = loudness * jnp.repeat(jnp.exp(draws), shape[position] // parts).reshape((-1,) + (1,) * (len(shape) - 1 - position))
    return loudness


def scatter_about(own_key, extent, scale, reach, cuts=(), dtype=jnp.bfloat16):
    factor_of = block_levels(own_key, extent, cuts, -0.22, 0.18) if cuts else 1.0
    array = jax.random.normal(own_key, extent, jnp.float32) * scale * factor_of
    return jnp.minimum(jnp.maximum(array, -reach), reach).astype(dtype)


def setup_inputs(seed: int = 0) -> dict:
    splits = jax.random.split(jax.random.key(seed), 6)
    return {
        "walkers": scatter_about(splits[0], (WALKERS, 2 * NOCC, NORB), 1.0, 6.0, ((0, 32),)),
        "inv_intersection": scatter_about(splits[1], (WALKERS, 2, NOCC, NOCC), NOCC ** -0.5, 0.625, ((0, 32),)),
        "rotated_chol": scatter_about(splits[2], (CHOL, NOCC, NORB), (NOCC * NORB) ** -0.5, 0.013671875, ((0, 8),)),
        "full_chol": scatter_about(splits[3], (CHOL, NORB, NORB), NORB ** -0.5, 0.125, ((0, 4), (1, 8))),
        "field_noise": scatter_about(splits[4], (CHOL,), 1.0, 4.0, (), jnp.float32),
    }


def reference(walkers, inv_intersection, rotated_chol, full_chol, field_noise):
    spins = walkers.reshape(WALKERS, 2, NOCC, NORB)
    theta = jnp.einsum('wsij,wsjp->wip', inv_intersection.astype(jnp.float32), spins.astype(jnp.float32)).astype(jnp.bfloat16)
    force_bias = jnp.einsum('wip,gip->wg', theta.astype(jnp.float32), rotated_chol.astype(jnp.float32))
    bias_shift = lax.optimization_barrier(jnp.sum(force_bias, axis=0)) / jnp.sqrt(jnp.float32(WALKERS))
    shifted = field_noise - bias_shift
    field = 0.1 * jnp.einsum('g,gij->ij', shifted, full_chol.astype(jnp.float32), precision=lax.Precision.HIGHEST)
    field = field.astype(jnp.bfloat16)
    current = walkers.reshape(WALKERS * 2 * NOCC, NORB)
    total = current.astype(jnp.float32)
    for order in range(1, 5):
        current = (jnp.dot(current, field, preferred_element_type=jnp.float32) / order).astype(jnp.bfloat16)
        total = total + current.astype(jnp.float32)
    propagated = total.astype(jnp.bfloat16).reshape(WALKERS, 2 * NOCC, NORB)
    return (propagated, force_bias, bias_shift)
```

```python
import functools
import math

import jax
import jax.numpy as jnp
from jax import lax
from jax.experimental import pallas as pl
from jax.experimental.pallas import tpu as pltpu
from jax.sharding import PartitionSpec as P

time_root = 0.1
orders = 4
f32, bf16 = jnp.float32, jnp.bfloat16


class Gather:
    def __init__(self, nb, chunks, ref_at, many, recv, send_f, send_s, send_b):
        self.nb, self.chunks, self.ref_at, self.many = nb, chunks, ref_at, many
        self.recv, self.send_f, self.send_s, self.send_b = recv, send_f, send_s, send_b
        me = lax.axis_index("blk")
        self.me, self.core = me, me % 2
        self.cols = 2 if nb % 4 == 0 else 1
        self.rows = nb // 2 // self.cols
        chip = me // 2
        col, row = chip % self.cols, chip // self.cols
        self.turn = self.core if self.rows == self.cols else 0
        self.f = (1 - self.turn) * col + self.turn * row
        self.s = (1 - self.turn) * row + self.turn * col
        self.nf, self.ns = self.cols, self.rows
        self.sibling = chip * 2 + 1 - self.core

    def at(self, i, j, core=None):
        f, s = (self.f + i) % self.nf, (self.s + j) % self.ns
        chip = (1 - self.turn) * (s * self.cols + f) + self.turn * (f * self.cols + s)
        return chip * 2 + (self.core if core is None else core)

    def copy(self, block, chunk, target, send):
        piece = self.ref_at(block, chunk)
        return pltpu.make_async_remote_copy(
            src_ref=piece, dst_ref=piece, send_sem=send, recv_sem=self.recv.at[block, chunk],
            device_id={"blk": target}, device_id_type=pl.DeviceIdType.MESH)

    def landed(self, block, chunk):
        self.copy(block, chunk, self.sibling, self.send_b).wait_recv()

    def own(self, chunk):
        for i in range(1, self.nf):
            self.copy(self.me, chunk, self.at(i, 0), self.send_f).start()
        for j in range(1, self.ns):
            self.copy(self.me, chunk, self.at(0, j), self.send_s).start()
        self.copy(self.me, chunk, self.sibling, self.send_b).start()

    def first(self, chunk):
        for i in range(1, self.nf):
            block = self.at(i, 0)
            self.landed(block, chunk)
            for j in range(1, self.ns):
                self.copy(block, chunk, self.at(0, j), self.send_s).start()
            self.copy(block, chunk, self.sibling, self.send_b).start()

    def second(self, chunk):
        for j in range(1, self.ns):
            for i in range(self.nf):
                block = self.at(i, j)
                self.landed(block, chunk)
                self.copy(block, chunk, self.sibling, self.send_b).start()

    def drain(self):
        for send, count in ((self.send_f, self.nf - 1), (self.send_s, (self.ns - 1) * self.nf), (self.send_b, self.nb // 2)):
            if count:
                piece = self.many(count)
                pltpu.make_async_remote_copy(
                    src_ref=piece, dst_ref=piece, send_sem=send, recv_sem=self.recv.at[0, 0],
                    device_id={"blk": self.sibling}, device_id_type=pl.DeviceIdType.MESH).wait_send()


def kernel(nb, nw, total_walkers, chunks, flat, three, inv, rot_hbm, full_hbm, noise,
           out, fb, shift,
           rot, full, theta, acc, field, mid, outer_in, inner_in, slots_w, slots_b, current, total,
           rot_recv, rot_f, rot_s, rot_b, fld_recv, fld_f, fld_s, fld_b,
           load, slot_send, slot_recv, in_send, in_recv, mid_send, mid_recv, out_send, out_recv):
    blk, walk = lax.axis_index("blk"), lax.axis_index("walk")
    wdev, occupied, orbitals = theta.shape
    per, group = rot_hbm.shape[0], rot.shape[0]
    local_count, block_rows = full_hbm.shape[0], full_hbm.shape[1]
    size = block_rows // chunks
    MESH = pl.DeviceIdType.MESH

    load_rot = pltpu.make_async_copy(rot_hbm, rot.at[pl.ds(blk * per, per)], load.at[0])
    load_rot.start()
    load_full = pltpu.make_async_copy(full_hbm, full, load.at[1])
    load_full.start()
    barrier = pltpu.get_barrier_semaphore()
    for d in range(1, nb):
        pl.semaphore_signal(barrier, inc=1, device_id={"blk": (blk + d) % nb}, device_id_type=MESH)
    for d in range(1, nw):
        pl.semaphore_signal(barrier, inc=1, device_id={"walk": (walk + d) % nw}, device_id_type=MESH)
    pl.semaphore_wait(barrier, nb + nw - 2)
    load_rot.wait()

    vectors = Gather(nb, per, lambda block, c: rot.at[block * per + c], lambda k: rot.at[pl.ds(0, k * per)],
                     rot_recv, rot_f, rot_s, rot_b)
    for c in range(per):
        vectors.own(c)

    tile = 512
    for w in range(wdev):
        for lo in range(0, orbitals, tile):
            theta[w, :, lo:lo + tile] = jnp.dot(inv[w], three[w, :, lo:lo + tile], preferred_element_type=f32).astype(bf16)

    def bias(g):
        for lo in range(0, orbitals, 256):
            vector = rot[g, :, lo:lo + 256].astype(f32)
            for w in range(wdev):
                product = vector * theta[w, :, lo:lo + 256].astype(f32)
                acc[pl.ds(w * group + g, 1), lo:lo + 256] = jnp.sum(product, axis=0, keepdims=True)

    def bias_block(block):
        @pl.loop(0, per)
        def _(c):
            bias(block * per + c)

    bias_block(blk)
    for c in range(per):
        vectors.first(c)
    for i in range(1, vectors.nf):
        bias_block(vectors.at(i, 0))
    for c in range(per):
        vectors.landed(vectors.sibling, c)
    bias_block(vectors.sibling)
    for c in range(per):
        vectors.second(c)
    for j in range(1, vectors.ns):
        for i in range(vectors.nf):
            bias_block(vectors.at(i, j))

    @pl.loop(1, nb // 2)
    def _(d):
        block = (vectors.sibling + 2 * d) % nb
        for c in range(per):
            vectors.landed(block, c)
        bias_block(block)

    biases = jnp.sum(acc[...], axis=1, keepdims=True)
    fb[...] = jnp.broadcast_to(biases, fb.shape)
    part = biases[0:group]
    for w in range(1, wdev):
        part = part + biases[w * group:(w + 1) * group]
    diagonal = lax.broadcasted_iota(jnp.int32, (group, 128), 0) == lax.broadcasted_iota(jnp.int32, (group, 128), 1)
    line = jnp.sum(jnp.where(diagonal, jnp.broadcast_to(part, (group, 128)), 0.0), axis=0, keepdims=True)
    for axis, count, me, slots, k in (("walk", nw, walk, slots_w, 0), ("blk", nb, blk, slots_b, 1)):
        slots[pl.ds(me, 1)] = line[None]
        if count > 1:
            for d in range(1, count):
                pltpu.make_async_remote_copy(
                    src_ref=slots.at[me], dst_ref=slots.at[me], send_sem=slot_send.at[k], recv_sem=slot_recv.at[k],
                    device_id={axis: (me + d) % count}, device_id_type=MESH).start()
            rest = slots.at[pl.ds(0, count - 1)]
            every = pltpu.make_async_remote_copy(
                src_ref=rest, dst_ref=rest, send_sem=slot_send.at[k], recv_sem=slot_recv.at[k],
                device_id={axis: (me + 1) % count}, device_id_type=MESH)
            every.wait()
        line = slots[0]
        for d in range(1, count):
            line = line + slots[d]
    shifts = line / math.sqrt(total_walkers)
    shift[...] = shifts
    shifted = (noise[...] - shifts[:, 0:group]) * time_root
    lane = lax.broadcasted_iota(jnp.int32, (1, group), 1)
    weights = [jnp.sum(jnp.where(lane == walk * local_count + j, shifted, 0.0), axis=1, keepdims=True)
               for j in range(local_count)]
    load_full.wait()

    half = nw // 2
    low = walk < half
    is_mid = (walk == half - 1) | (walk == half)
    has_outer = (walk != 0) & (walk != nw - 1)
    step = 1 - 2 * (walk >= half).astype(jnp.int32)
    inward = (walk + step + nw) % nw
    outward = (walk - step + nw) % nw
    lag = jnp.where(is_mid, 1, 3)
    rows = lambda block, c: field.at[pl.ds(pl.multiple_of(block * block_rows + c * size, size), size)]
    gather = Gather(nb, chunks, rows, lambda k: field.at[pl.ds(0, k * block_rows)], fld_recv, fld_f, fld_s, fld_b)

    def hop(src, dst, send, recv, target):
        return pltpu.make_async_remote_copy(src_ref=src, dst_ref=dst, send_sem=send, recv_sem=recv,
                                            device_id={"walk": target}, device_id_type=MESH)

    def to_mid(c):
        return hop(mid.at[c], outer_in.at[c], in_send.at[c], in_recv.at[c], inward)

    def across(c):
        return hop(mid.at[c], inner_in.at[c], mid_send.at[c], mid_recv.at[c], inward)

    def back(c):
        return hop(rows(blk, c), rows(blk, c), out_send.at[c], out_recv.at[c], outward)

    def reduce_in(c):
        span = pl.ds(pl.multiple_of(c * size, size), size)

        def summed():
            value = weights[0] * full[0, span, :].astype(f32)
            for j in range(1, local_count):
                value = value + weights[j] * full[j, span, :].astype(f32)
            return value

        @pl.when(has_outer)
        def _():
            to_mid(c).wait_recv()
            mid[c] = (summed() + outer_in[c].astype(f32)).astype(bf16)

        @pl.when(jnp.logical_not(has_outer))
        def _():
            mid[c] = summed().astype(bf16)

        @pl.when(is_mid)
        def _():
            across(c).start()

        @pl.when(jnp.logical_not(is_mid))
        def _():
            to_mid(c).start()

    def spread(c):
        @pl.when(is_mid)
        def _():
            across(c).wait_recv()
            span = pl.ds(pl.multiple_of(blk * block_rows + c * size, size), size)
            field[span, :] = (mid[c].astype(f32) + inner_in[c].astype(f32)).astype(bf16)

        @pl.when(jnp.logical_not(is_mid))
        def _():
            back(c).wait_recv()

        @pl.when(has_outer)
        def _():
            back(c).start()

        gather.own(c)

    def when_chunk(c, action):
        @pl.when((c >= 0) & (c < chunks))
        def _():
            action(c)

    @pl.loop(0, chunks + 5)
    def _(t):
        when_chunk(t, reduce_in)
        when_chunk(t - lag, spread)
        when_chunk(t - lag - 1, gather.first)
        when_chunk(t - lag - 2, gather.second)

    @pl.loop(0, nb // 2)
    def _(d):
        @pl.loop(0, chunks)
        def _(c):
            gather.landed((gather.sibling + 2 * d) % nb, c)

    source = flat
    for order in range(1, orders + 1):
        target = current.at[order % 2]

        @pl.loop(0, orbitals // tile)
        def _(n):
            span = pl.ds(pl.multiple_of(n * tile, tile), tile)
            term = (jnp.dot(source[...], field[:, span], preferred_element_type=f32) / order).astype(bf16)
            before = flat[:, span].astype(f32) if order == 1 else total[:, span]
            after = before + term.astype(f32)
            if order == orders:
                out[:, span] = after.astype(bf16)
            else:
                target[:, span] = term
                total[:, span] = after

        source = target

    vectors.drain()
    gather.drain()

    @pl.loop(0, chunks)
    def _(c):
        @pl.when(is_mid)
        def _():
            across(c).wait_send()

        @pl.when(jnp.logical_not(is_mid))
        def _():
            to_mid(c).wait_send()

        @pl.when(has_outer)
        def _():
            back(c).wait_send()


def local(nb, nw, walkers, inv_intersection, rotated_chol, full_chol, field_noise):
    wdev, double_rows, orbitals = walkers.shape
    occupied = double_rows // 2
    group = field_noise.shape[0]
    per = rotated_chol.shape[0]
    local_count, block_rows, _ = full_chol.shape
    chunks = 8
    size = block_rows // chunks
    flat = walkers.reshape(wdev * double_rows, orbitals)
    inv = inv_intersection.transpose(0, 2, 1, 3).reshape(wdev, occupied, double_rows)
    vmem, hbm = pl.BlockSpec(memory_space=pltpu.VMEM), pl.BlockSpec(memory_space=pl.ANY)
    dma = pltpu.SemaphoreType.DMA
    out, fb, shift = pl.pallas_call(
        functools.partial(kernel, nb, nw, wdev * nb * nw, chunks),
        out_shape=(jax.ShapeDtypeStruct(flat.shape, bf16), jax.ShapeDtypeStruct((wdev * group, 128), f32),
                   jax.ShapeDtypeStruct((1, 128), f32)),
        in_specs=[vmem, vmem, vmem, hbm, hbm, vmem],
        out_specs=(vmem, vmem, vmem),
        scratch_shapes=[
            pltpu.VMEM((group, occupied, orbitals), bf16),
            pltpu.VMEM(full_chol.shape, bf16),
            pltpu.VMEM((wdev, occupied, orbitals), bf16),
            pltpu.VMEM((wdev * group, orbitals), f32),
            pltpu.VMEM((orbitals, orbitals), bf16),
            pltpu.VMEM((chunks, size, orbitals), bf16),
            pltpu.VMEM((chunks, size, orbitals), bf16),
            pltpu.VMEM((chunks, size, orbitals), bf16),
            pltpu.VMEM((nw, 1, 128), f32),
            pltpu.VMEM((nb, 1, 128), f32),
            pltpu.VMEM((2,) + flat.shape, bf16),
            pltpu.VMEM(flat.shape, f32),
            dma((nb, per)), dma, dma, dma,
            dma((nb, chunks)), dma, dma, dma,
            dma((2,)), dma((2,)), dma((2,)),
            dma((chunks,)), dma((chunks,)), dma((chunks,)), dma((chunks,)), dma((chunks,)), dma((chunks,)),
        ],
        compiler_params=pltpu.CompilerParams(collective_id=0, has_side_effects=True, vmem_limit_bytes=60 * 2**20),
    )(flat, walkers, inv, rotated_chol, full_chol, field_noise.reshape(1, group))
    return (out.reshape(walkers.shape), fb[:, 0].reshape(wdev, group), shift[0, :group])


def solution(mesh):
    placed = (
        P(("blk", "walk"), None, None),
        P(("blk", "walk"), None, None, None),
        P("blk", None, None),
        P("walk", "blk", None),
        P(),
    )
    return jax.shard_map(
        functools.partial(local, mesh.shape["blk"], mesh.shape["walk"]),
        mesh=mesh,
        in_specs=placed,
        out_specs=(P(("blk", "walk"), None, None), P(("blk", "walk"), None), P()),
        check_vma=False,
    )
```

```python
import functools
import math

import jax
import jax.numpy as jnp
from jax import lax
from jax.experimental import pallas as pl
from jax.experimental.pallas import tpu as pltpu
from jax.sharding import PartitionSpec as P

time_root = 0.1
orders = 4
f32, bf16 = jnp.float32, jnp.bfloat16


class Gather:
    def __init__(self, nb, chunks, ref_at, many, recv, send_f, send_s, send_b):
        self.nb, self.chunks, self.ref_at, self.many = nb, chunks, ref_at, many
        self.recv, self.send_f, self.send_s, self.send_b = recv, send_f, send_s, send_b
        me = lax.axis_index("blk")
        self.me, self.core = me, me % 2
        self.cols = 2 if nb % 4 == 0 else 1
        self.rows = nb // 2 // self.cols
        chip = me // 2
        col, row = chip % self.cols, chip // self.cols
        self.turn = self.core if self.rows == self.cols else 0
        self.f = (1 - self.turn) * col + self.turn * row
        self.s = (1 - self.turn) * row + self.turn * col
        self.nf, self.ns = self.cols, self.rows
        self.sibling = chip * 2 + 1 - self.core

    def at(self, i, j, core=None):
        f, s = (self.f + i) % self.nf, (self.s + j) % self.ns
        chip = (1 - self.turn) * (s * self.cols + f) + self.turn * (f * self.cols + s)
        return chip * 2 + (self.core if core is None else core)

    def copy(self, block, chunk, target, send):
        piece = self.ref_at(block, chunk)
        return pltpu.make_async_remote_copy(
            src_ref=piece, dst_ref=piece, send_sem=send, recv_sem=self.recv.at[block, chunk],
            device_id={"blk": target}, device_id_type=pl.DeviceIdType.MESH)

    def landed(self, block, chunk):
        self.copy(block, chunk, self.sibling, self.send_b).wait_recv()

    def own(self, chunk):
        self.far(chunk)
        self.near(chunk)

    def far(self, chunk):
        for i in range(1, self.nf):
            self.copy(self.me, chunk, self.at(i, 0), self.send_f).start()
        for j in range(1, self.ns):
            self.copy(self.me, chunk, self.at(0, j), self.send_s).start()

    def near(self, chunk):
        self.copy(self.me, chunk, self.sibling, self.send_b).start()

    def first(self, chunk):
        for i in range(1, self.nf):
            block = self.at(i, 0)
            self.landed(block, chunk)
            for j in range(1, self.ns):
                self.copy(block, chunk, self.at(0, j), self.send_s).start()
            self.copy(block, chunk, self.sibling, self.send_b).start()

    def second(self, chunk):
        for j in range(1, self.ns):
            for i in range(self.nf):
                block = self.at(i, j)
                self.landed(block, chunk)
                self.copy(block, chunk, self.sibling, self.send_b).start()

    def drain(self):
        for send, count in ((self.send_f, self.nf - 1), (self.send_s, (self.ns - 1) * self.nf), (self.send_b, self.nb // 2)):
            if count:
                piece = self.many(count)
                pltpu.make_async_remote_copy(
                    src_ref=piece, dst_ref=piece, send_sem=send, recv_sem=self.recv.at[0, 0],
                    device_id={"blk": self.sibling}, device_id_type=pl.DeviceIdType.MESH).wait_send()


def kernel(nb, nw, total_walkers, chunks, split, flat, three, inv, rot_hbm, full_hbm, noise,
           out, fb, shift,
           pair, mine, zout, zin, pin, rot, full, theta, acc, field, mid, outer_in, inner_in, slots_w, slots_b, current, total,
           rot_recv, rot_f, rot_s, rot_b, fld_recv, fld_f, fld_s, fld_b,
           load, slot_send, slot_recv, in_send, in_recv, mid_send, mid_recv, out_send, out_recv):
    blk, walk = lax.axis_index("blk"), lax.axis_index("walk")
    wdev, occupied, orbitals = theta.shape
    per, group = rot_hbm.shape[0], rot.shape[0]
    local_count, block_rows = full_hbm.shape[0], full_hbm.shape[1]
    size = block_rows // chunks
    MESH = pl.DeviceIdType.MESH

    load_rot = pltpu.make_async_copy(rot_hbm, rot.at[pl.ds(blk * per, per)], load.at[0])
    load_rot.start()
    load_full = pltpu.make_async_copy(full_hbm, full, load.at[1])
    load_full.start()
    barrier = pltpu.get_barrier_semaphore()
    for d in range(1, nb):
        pl.semaphore_signal(barrier, inc=1, device_id={"blk": (blk + d) % nb}, device_id_type=MESH)
    for d in range(1, nw):
        pl.semaphore_signal(barrier, inc=1, device_id={"walk": (walk + d) % nw}, device_id_type=MESH)
    pl.semaphore_wait(barrier, nb + nw - 2)
    load_rot.wait()

    vectors = Gather(nb, per, lambda block, c: rot.at[block * per + c], lambda k: rot.at[pl.ds(0, k * per)],
                     rot_recv, rot_f, rot_s, rot_b)
    vectors.far(0)
    for c in range(per):
        vectors.near(c)

    def share(slots, source, me, peers, k):
        for peer, slot in peers:
            pltpu.make_async_remote_copy(
                src_ref=slots.at[me] if source is None else source.at[slot], dst_ref=slots.at[me],
                send_sem=slot_send.at[k], recv_sem=slot_recv.at[k], device_id=peer, device_id_type=MESH).start()

        def finish():
            rest = slots.at[pl.ds(0, len(peers))]
            pltpu.make_async_remote_copy(
                src_ref=rest, dst_ref=rest, send_sem=slot_send.at[k], recv_sem=slot_recv.at[k],
                device_id=peers[0][0], device_id_type=MESH).wait()

        return finish

    walk_peers = [({"walk": (walk + d) % nw}, (walk + d) % nw) for d in range(1, nw)]
    blk_peers = [({"blk": (blk + d) % nb}, (blk + d) % nb) for d in range(1, nb)]
    tile = 512
    parts, span_width = (2, pair.shape[-1]) if split else (1, orbitals)

    def project(begin, into):
        for lo in range(0, span_width, tile):
            span = pl.ds(pl.multiple_of(begin + lo, tile), tile)
            both = jnp.zeros((occupied, tile), f32)
            for w in range(wdev):
                one = jnp.dot(inv[w], three[w, :, span], preferred_element_type=f32).astype(bf16)
                theta[w, :, span] = one
                both = both + one.astype(f32)
            into[:, lo:lo + tile] = both

    first_column = 0
    if split:
        project((1 - vectors.core) * span_width, pair.at[0])
        swap = pltpu.make_async_remote_copy(
            src_ref=pair.at[0], dst_ref=pair.at[1], send_sem=slot_send.at[4], recv_sem=slot_recv.at[4],
            device_id={"blk": vectors.sibling}, device_id_type=MESH)
        swap.start()
        first_column = vectors.core * span_width
        project(first_column, mine)
        swap.wait()
    else:
        project(0, mine)
    width = span_width // nw
    for k in range(nw):
        value = mine[:, k * width:(k + 1) * width]
        if split:
            value = value + pair[1, :, k * width:(k + 1) * width]
        zout[k] = value.astype(bf16)
    zin[pl.ds(walk, 1)] = zout[pl.ds(walk, 1)]
    share(zin, zout, walk, walk_peers, 2)()
    value = zin[0].astype(f32)
    for k in range(1, nw):
        value = value + zin[k].astype(f32)
    if split:
        place = blk // 2
        plane_peers = [({"blk": (blk + 2 * d) % nb}, 0) for d in range(1, nb // 2)]
    else:
        place, plane_peers = blk, blk_peers
    pin[pl.ds(place, 1)] = value.astype(bf16)[None]
    finish = share(pin, None, place, plane_peers, 3)
    for c in range(1, per):
        vectors.far(c)
    for c in range(per):
        vectors.landed(vectors.sibling, c)
    finish()
    value = pin[0].astype(f32)
    for k in range(1, pin.shape[0]):
        value = value + pin[k].astype(f32)
    columns = pl.ds(pl.multiple_of(first_column + walk * width, width), width)
    spot = lax.broadcasted_iota(jnp.int32, (1, 128), 1)
    line = jnp.zeros((1, 128), f32)
    for c in range(per * parts):
        g = place * per * parts + c
        product = rot[g, :, columns].astype(f32) * value
        one = jnp.sum(jnp.sum(product, axis=0, keepdims=True), axis=1, keepdims=True)
        line = line + jnp.where(spot == g, one, 0.0)
    for peers, me, slots, k in ((walk_peers, walk, slots_w, 0), (blk_peers, blk, slots_b, 1)):
        slots[pl.ds(me, 1)] = line[None]
        share(slots, None, me, peers, k)()
        line = slots[0]
        for d in range(1, slots.shape[0]):
            line = line + slots[d]
    shifts = line / math.sqrt(total_walkers)
    shift[...] = shifts[:, 0:group]
    shifted = (noise[...] - shifts[:, 0:group]) * time_root
    lane = lax.broadcasted_iota(jnp.int32, (1, group), 1)
    weights = [jnp.sum(jnp.where(lane == walk * local_count + j, shifted, 0.0), axis=1, keepdims=True)
               for j in range(local_count)]
    load_full.wait()

    half = nw // 2
    low = walk < half
    is_mid = (walk == half - 1) | (walk == half)
    has_outer = (walk != 0) & (walk != nw - 1)
    step = 1 - 2 * (walk >= half).astype(jnp.int32)
    inward = (walk + step + nw) % nw
    outward = (walk - step + nw) % nw
    lag = jnp.where(is_mid, 1, 3)
    rows = lambda block, c: field.at[pl.ds(pl.multiple_of(block * block_rows + c * size, size), size)]
    gather = Gather(nb, chunks, rows, lambda k: field.at[pl.ds(0, k * block_rows)], fld_recv, fld_f, fld_s, fld_b)

    def hop(src, dst, send, recv, target):
        return pltpu.make_async_remote_copy(src_ref=src, dst_ref=dst, send_sem=send, recv_sem=recv,
                                            device_id={"walk": target}, device_id_type=MESH)

    def to_mid(c):
        return hop(mid.at[c], outer_in.at[c], in_send.at[c], in_recv.at[c], inward)

    def across(c):
        return hop(mid.at[c], inner_in.at[c], mid_send.at[c], mid_recv.at[c], inward)

    def back(c):
        return hop(rows(blk, c), rows(blk, c), out_send.at[c], out_recv.at[c], outward)

    def reduce_in(c):
        span = pl.ds(pl.multiple_of(c * size, size), size)

        def summed():
            value = weights[0] * full[0, span, :].astype(f32)
            for j in range(1, local_count):
                value = value + weights[j] * full[j, span, :].astype(f32)
            return value

        @pl.when(has_outer)
        def _():
            to_mid(c).wait_recv()
            mid[c] = (summed() + outer_in[c].astype(f32)).astype(bf16)

        @pl.when(jnp.logical_not(has_outer))
        def _():
            mid[c] = summed().astype(bf16)

        @pl.when(is_mid)
        def _():
            across(c).start()

        @pl.when(jnp.logical_not(is_mid))
        def _():
            to_mid(c).start()

    def spread(c):
        @pl.when(is_mid)
        def _():
            across(c).wait_recv()
            span = pl.ds(pl.multiple_of(blk * block_rows + c * size, size), size)
            field[span, :] = (mid[c].astype(f32) + inner_in[c].astype(f32)).astype(bf16)

        @pl.when(jnp.logical_not(is_mid))
        def _():
            back(c).wait_recv()

        @pl.when(has_outer)
        def _():
            back(c).start()

        gather.own(c)

    def when_chunk(c, action):
        @pl.when((c >= 0) & (c < chunks))
        def _():
            action(c)

    def bias(g):
        for lo in range(0, orbitals, 256):
            vector = rot[g, :, lo:lo + 256].astype(f32)
            for w in range(wdev):
                product = vector * theta[w, :, lo:lo + 256].astype(f32)
                acc[pl.ds(w * group + g, 1), lo:lo + 256] = jnp.sum(product, axis=0, keepdims=True)

    def bias_block(block):
        @pl.loop(0, per)
        def _(c):
            bias(block * per + c)

    def vectors_first():
        bias_block(blk)
        bias_block(vectors.sibling)
        for i in range(1, vectors.nf):
            bias_block(vectors.at(i, 0))

    def vectors_second():
        for c in range(per):
            vectors.second(c)
        for j in range(1, vectors.ns):
            for i in range(vectors.nf):
                bias_block(vectors.at(i, j))

    def vectors_third():
        @pl.loop(1, nb // 2)
        def _(d):
            block = (vectors.sibling + 2 * d) % nb
            for c in range(per):
                vectors.landed(block, c)
            bias_block(block)

    for c in range(per):
        vectors.first(c)

    @pl.loop(0, chunks + 5)
    def _(t):
        when_chunk(t, reduce_in)
        when_chunk(t - lag, spread)
        when_chunk(t - lag - 1, gather.first)
        when_chunk(t - lag - 2, gather.second)
        pl.when(t == lag)(vectors_first)
        pl.when(t == lag + 2)(vectors_second)
        pl.when(t == lag + 4)(vectors_third)

    biases = jnp.sum(acc[...], axis=1, keepdims=True)
    diagonal = lax.broadcasted_iota(jnp.int32, (group, group), 0) == lax.broadcasted_iota(jnp.int32, (group, group), 1)
    for w in range(wdev):
        column = jnp.broadcast_to(biases[w * group:(w + 1) * group], (group, group))
        fb[w:w + 1, :] = jnp.sum(jnp.where(diagonal, column, 0.0), axis=0, keepdims=True)

    @pl.loop(0, nb // 2)
    def _(d):
        @pl.loop(0, chunks)
        def _(c):
            gather.landed((gather.sibling + 2 * d) % nb, c)

    source = flat
    for order in range(1, orders + 1):
        target = current.at[order % 2]

        @pl.loop(0, orbitals // tile)
        def _(n):
            span = pl.ds(pl.multiple_of(n * tile, tile), tile)
            term = (jnp.dot(source[...], field[:, span], preferred_element_type=f32) / order).astype(bf16)
            before = flat[:, span].astype(f32) if order == 1 else total[:, span]
            after = before + term.astype(f32)
            if order == orders:
                out[:, span] = after.astype(bf16)
            else:
                target[:, span] = term
                total[:, span] = after

        source = target

    vectors.drain()
    gather.drain()

    @pl.loop(0, chunks)
    def _(c):
        @pl.when(is_mid)
        def _():
            across(c).wait_send()

        @pl.when(jnp.logical_not(is_mid))
        def _():
            to_mid(c).wait_send()

        @pl.when(has_outer)
        def _():
            back(c).wait_send()


def local(nb, nw, walkers, inv_intersection, rotated_chol, full_chol, field_noise):
    wdev, double_rows, orbitals = walkers.shape
    occupied = double_rows // 2
    group = field_noise.shape[0]
    per = rotated_chol.shape[0]
    local_count, block_rows, _ = full_chol.shape
    chunks = 8
    size = block_rows // chunks
    split = orbitals // 2 // nw % 128 == 0
    half = orbitals // 2 if split else orbitals
    flat = walkers.reshape(wdev * double_rows, orbitals)
    inv = inv_intersection.transpose(0, 2, 1, 3).reshape(wdev, occupied, double_rows)
    vmem, hbm = pl.BlockSpec(memory_space=pltpu.VMEM), pl.BlockSpec(memory_space=pl.ANY)
    dma = pltpu.SemaphoreType.DMA
    out, fb, shift = pl.pallas_call(
        functools.partial(kernel, nb, nw, wdev * nb * nw, chunks, split),
        out_shape=(jax.ShapeDtypeStruct(flat.shape, bf16), jax.ShapeDtypeStruct((wdev, group), f32),
                   jax.ShapeDtypeStruct((1, group), f32)),
        in_specs=[vmem, vmem, vmem, hbm, hbm, vmem],
        out_specs=(vmem, vmem, vmem),
        scratch_shapes=[
            pltpu.VMEM((2, occupied, half), f32),
            pltpu.VMEM((occupied, half), f32),
            pltpu.VMEM((nw, occupied, half // nw), bf16),
            pltpu.VMEM((nw, occupied, half // nw), bf16),
            pltpu.VMEM((nb // 2 if split else nb, occupied, half // nw), bf16),
            pltpu.VMEM((group, occupied, orbitals), bf16),
            pltpu.VMEM(full_chol.shape, bf16),
            pltpu.VMEM((wdev, occupied, orbitals), bf16),
            pltpu.VMEM((wdev * group, orbitals), f32),
            pltpu.VMEM((orbitals, orbitals), bf16),
            pltpu.VMEM((chunks, size, orbitals), bf16),
            pltpu.VMEM((chunks, size, orbitals), bf16),
            pltpu.VMEM((chunks, size, orbitals), bf16),
            pltpu.VMEM((nw, 1, 128), f32),
            pltpu.VMEM((nb, 1, 128), f32),
            pltpu.VMEM((2,) + flat.shape, bf16),
            pltpu.VMEM(flat.shape, f32),
            dma((nb, per)), dma, dma, dma,
            dma((nb, chunks)), dma, dma, dma,
            dma((2,)), dma((5,)), dma((5,)),
            dma((chunks,)), dma((chunks,)), dma((chunks,)), dma((chunks,)), dma((chunks,)), dma((chunks,)),
        ],
        compiler_params=pltpu.CompilerParams(collective_id=0, has_side_effects=True, vmem_limit_bytes=60 * 2**20),
    )(flat, walkers, inv, rotated_chol, full_chol, field_noise.reshape(1, group))
    return (out.reshape(walkers.shape), fb, shift.reshape(group))


def solution(mesh):
    placed = (
        P(("blk", "walk"), None, None),
        P(("blk", "walk"), None, None, None),
        P("blk", None, None),
        P("walk", "blk", None),
        P(),
    )
    return jax.shard_map(
        functools.partial(local, mesh.shape["blk"], mesh.shape["walk"]),
        mesh=mesh,
        in_specs=placed,
        out_specs=(P(("blk", "walk"), None, None), P(("blk", "walk"), None), P()),
        check_vma=False,
    )
```

```python
import functools
import math

import jax
import jax.numpy as jnp
from jax import lax
from jax.experimental import pallas as pl
from jax.experimental.pallas import tpu as pltpu
from jax.sharding import PartitionSpec as P

time_root = 0.1
orders = 4
f32, bf16 = jnp.float32, jnp.bfloat16


class Gather:
    def __init__(self, nb, chunks, ref_at, many, recv, send_f, send_s, send_b):
        self.nb, self.chunks, self.ref_at, self.many = nb, chunks, ref_at, many
        self.recv, self.send_f, self.send_s, self.send_b = recv, send_f, send_s, send_b
        me = lax.axis_index("blk")
        self.me, self.core = me, me % 2
        self.cols = 2 if nb % 4 == 0 else 1
        self.rows = nb // 2 // self.cols
        chip = me // 2
        col, row = chip % self.cols, chip // self.cols
        self.turn = self.core if self.rows == self.cols else 0
        self.f = (1 - self.turn) * col + self.turn * row
        self.s = (1 - self.turn) * row + self.turn * col
        self.nf, self.ns = self.cols, self.rows
        self.sibling = chip * 2 + 1 - self.core

    def at(self, i, j, core=None):
        f, s = (self.f + i) % self.nf, (self.s + j) % self.ns
        chip = (1 - self.turn) * (s * self.cols + f) + self.turn * (f * self.cols + s)
        return chip * 2 + (self.core if core is None else core)

    def copy(self, block, chunk, target, send):
        piece = self.ref_at(block, chunk)
        return pltpu.make_async_remote_copy(
            src_ref=piece, dst_ref=piece, send_sem=send, recv_sem=self.recv.at[block, chunk],
            device_id={"blk": target}, device_id_type=pl.DeviceIdType.MESH)

    def landed(self, block, chunk):
        self.copy(block, chunk, self.sibling, self.send_b).wait_recv()

    def own(self, chunk):
        self.far(chunk)
        self.near(chunk)

    def far(self, chunk):
        for i in range(1, self.nf):
            self.copy(self.me, chunk, self.at(i, 0), self.send_f).start()
        for j in range(1, self.ns):
            self.copy(self.me, chunk, self.at(0, j), self.send_s).start()

    def near(self, chunk):
        self.copy(self.me, chunk, self.sibling, self.send_b).start()

    def first(self, chunk):
        for i in range(1, self.nf):
            block = self.at(i, 0)
            self.landed(block, chunk)
            for j in range(1, self.ns):
                self.copy(block, chunk, self.at(0, j), self.send_s).start()
            self.copy(block, chunk, self.sibling, self.send_b).start()

    def second(self, chunk):
        for j in range(1, self.ns):
            for i in range(self.nf):
                block = self.at(i, j)
                self.landed(block, chunk)
                self.copy(block, chunk, self.sibling, self.send_b).start()

    def drain(self):
        for send, count in ((self.send_f, self.nf - 1), (self.send_s, (self.ns - 1) * self.nf), (self.send_b, self.nb // 2)):
            if count:
                piece = self.many(count)
                pltpu.make_async_remote_copy(
                    src_ref=piece, dst_ref=piece, send_sem=send, recv_sem=self.recv.at[0, 0],
                    device_id={"blk": self.sibling}, device_id_type=pl.DeviceIdType.MESH).wait_send()


def kernel(nb, nw, total_walkers, chunks, split, flat, three, inv, rot_hbm, full_hbm, noise,
           out, fb, shift,
           pair, mine, zout, zin, pin, rot, full, theta, acc, field, mid, outer_in, inner_in, slots_w, slots_b, terms,
           rot_recv, rot_f, rot_s, rot_b, fld_recv, fld_f, fld_s, fld_b,
           load, slot_send, slot_recv, in_send, in_recv, mid_send, mid_recv, out_send, out_recv):
    blk, walk = lax.axis_index("blk"), lax.axis_index("walk")
    wdev, occupied, orbitals = theta.shape
    per, group = rot_hbm.shape[0], rot.shape[0]
    local_count, block_rows = full_hbm.shape[0], full_hbm.shape[1]
    size = orbitals // chunks
    MESH = pl.DeviceIdType.MESH

    load_rot = pltpu.make_async_copy(rot_hbm, rot.at[pl.ds(blk * per, per)], load.at[0])
    load_rot.start()
    load_full = pltpu.make_async_copy(full_hbm, full, load.at[1])
    load_full.start()
    barrier = pltpu.get_barrier_semaphore()
    for d in range(1, nb):
        pl.semaphore_signal(barrier, inc=1, device_id={"blk": (blk + d) % nb}, device_id_type=MESH)
    for d in range(1, nw):
        pl.semaphore_signal(barrier, inc=1, device_id={"walk": (walk + d) % nw}, device_id_type=MESH)
    pl.semaphore_wait(barrier, nb + nw - 2)
    load_rot.wait()

    vectors = Gather(nb, per, lambda block, c: rot.at[block * per + c], lambda k: rot.at[pl.ds(0, k * per)],
                     rot_recv, rot_f, rot_s, rot_b)
    vectors.far(0)
    for c in range(per):
        vectors.near(c)

    def share(slots, source, me, peers, k):
        for peer, slot in peers:
            pltpu.make_async_remote_copy(
                src_ref=slots.at[me] if source is None else source.at[slot], dst_ref=slots.at[me],
                send_sem=slot_send.at[k], recv_sem=slot_recv.at[k], device_id=peer, device_id_type=MESH).start()

        def finish():
            rest = slots.at[pl.ds(0, len(peers))]
            pltpu.make_async_remote_copy(
                src_ref=rest, dst_ref=rest, send_sem=slot_send.at[k], recv_sem=slot_recv.at[k],
                device_id=peers[0][0], device_id_type=MESH).wait()

        return finish

    walk_peers = [({"walk": (walk + d) % nw}, (walk + d) % nw) for d in range(1, nw)]
    blk_peers = [({"blk": (blk + d) % nb}, (blk + d) % nb) for d in range(1, nb)]
    tile = 512
    parts, span_width = (2, pair.shape[-1]) if split else (1, orbitals)

    def project(begin, into):
        for lo in range(0, span_width, tile):
            span = pl.ds(pl.multiple_of(begin + lo, tile), tile)
            both = jnp.zeros((occupied, tile), f32)
            for w in range(wdev):
                one = jnp.dot(inv[w], three[w, :, span], preferred_element_type=f32).astype(bf16)
                theta[w, :, span] = one
                both = both + one.astype(f32)
            into[:, lo:lo + tile] = both

    first_column = 0
    if split:
        project((1 - vectors.core) * span_width, pair.at[0])
        swap = pltpu.make_async_remote_copy(
            src_ref=pair.at[0], dst_ref=pair.at[1], send_sem=slot_send.at[4], recv_sem=slot_recv.at[4],
            device_id={"blk": vectors.sibling}, device_id_type=MESH)
        swap.start()
        first_column = vectors.core * span_width
        project(first_column, mine)
        swap.wait()
    else:
        project(0, mine)
    width = span_width // nw
    for k in range(nw):
        value = mine[:, k * width:(k + 1) * width]
        if split:
            value = value + pair[1, :, k * width:(k + 1) * width]
        zout[k] = value.astype(bf16)
    zin[pl.ds(walk, 1)] = zout[pl.ds(walk, 1)]
    share(zin, zout, walk, walk_peers, 2)()
    value = zin[0].astype(f32)
    for k in range(1, nw):
        value = value + zin[k].astype(f32)
    if split:
        place = blk // 2
        plane_peers = [({"blk": (blk + 2 * d) % nb}, 0) for d in range(1, nb // 2)]
    else:
        place, plane_peers = blk, blk_peers
    pin[pl.ds(place, 1)] = value.astype(bf16)[None]
    finish = share(pin, None, place, plane_peers, 3)
    for c in range(1, per):
        vectors.far(c)
    for c in range(per):
        vectors.landed(vectors.sibling, c)
    finish()
    value = pin[0].astype(f32)
    for k in range(1, pin.shape[0]):
        value = value + pin[k].astype(f32)
    columns = pl.ds(pl.multiple_of(first_column + walk * width, width), width)
    spot = lax.broadcasted_iota(jnp.int32, (1, 128), 1)
    line = jnp.zeros((1, 128), f32)
    for c in range(per * parts):
        g = place * per * parts + c
        product = rot[g, :, columns].astype(f32) * value
        one = jnp.sum(jnp.sum(product, axis=0, keepdims=True), axis=1, keepdims=True)
        line = line + jnp.where(spot == g, one, 0.0)
    for peers, me, slots, k in ((walk_peers, walk, slots_w, 0), (blk_peers, blk, slots_b, 1)):
        slots[pl.ds(me, 1)] = line[None]
        share(slots, None, me, peers, k)()
        line = slots[0]
        for d in range(1, slots.shape[0]):
            line = line + slots[d]
    shifts = line / math.sqrt(total_walkers)
    shift[...] = shifts[:, 0:group]
    shifted = (noise[...] - shifts[:, 0:group]) * time_root
    lane = lax.broadcasted_iota(jnp.int32, (1, group), 1)
    weights = [jnp.sum(jnp.where(lane == walk * local_count + j, shifted, 0.0), axis=1, keepdims=True)
               for j in range(local_count)]
    load_full.wait()

    half = nw // 2
    low = walk < half
    is_mid = (walk == half - 1) | (walk == half)
    has_outer = (walk != 0) & (walk != nw - 1)
    step = 1 - 2 * (walk >= half).astype(jnp.int32)
    inward = (walk + step + nw) % nw
    outward = (walk - step + nw) % nw
    lag = jnp.where(is_mid, 1, 3)
    cols = lambda c: pl.ds(pl.multiple_of(c * size, size), size)
    rows = lambda block: pl.ds(pl.multiple_of(block * block_rows, block_rows), block_rows)
    part_at = lambda block, c: field.at[rows(block), cols(c)]
    gather = Gather(nb, chunks, part_at, lambda k: field.at[pl.ds(0, k * block_rows)], fld_recv, fld_f, fld_s, fld_b)

    def hop(src, dst, send, recv, target):
        return pltpu.make_async_remote_copy(src_ref=src, dst_ref=dst, send_sem=send, recv_sem=recv,
                                            device_id={"walk": target}, device_id_type=MESH)

    def to_mid(c):
        return hop(mid.at[c], outer_in.at[c], in_send.at[c], in_recv.at[c], inward)

    def across(c):
        return hop(mid.at[c], inner_in.at[c], mid_send.at[c], mid_recv.at[c], inward)

    def back(c):
        return hop(part_at(blk, c), part_at(blk, c), out_send.at[c], out_recv.at[c], outward)

    def reduce_in(c):
        def summed():
            value = weights[0] * full[0, :, cols(c)].astype(f32)
            for j in range(1, local_count):
                value = value + weights[j] * full[j, :, cols(c)].astype(f32)
            return value

        @pl.when(has_outer)
        def _():
            to_mid(c).wait_recv()
            mid[c] = (summed() + outer_in[c].astype(f32)).astype(bf16)

        @pl.when(jnp.logical_not(has_outer))
        def _():
            mid[c] = summed().astype(bf16)

        @pl.when(is_mid)
        def _():
            across(c).start()

        @pl.when(jnp.logical_not(is_mid))
        def _():
            to_mid(c).start()

    def spread(c):
        @pl.when(is_mid)
        def _():
            across(c).wait_recv()
            field[rows(blk), cols(c)] = (mid[c].astype(f32) + inner_in[c].astype(f32)).astype(bf16)

        @pl.when(jnp.logical_not(is_mid))
        def _():
            back(c).wait_recv()

        @pl.when(has_outer)
        def _():
            back(c).start()

        gather.own(c)

    def when_chunk(c, action):
        @pl.when((c >= 0) & (c < chunks))
        def _():
            action(c)

    def bias(g):
        for lo in range(0, orbitals, 256):
            vector = rot[g, :, lo:lo + 256].astype(f32)
            for w in range(wdev):
                product = vector * theta[w, :, lo:lo + 256].astype(f32)
                acc[pl.ds(w * group + g, 1), lo:lo + 256] = jnp.sum(product, axis=0, keepdims=True)

    def bias_block(block):
        @pl.loop(0, per)
        def _(c):
            bias(block * per + c)

    def vectors_first():
        bias_block(blk)
        bias_block(vectors.sibling)
        for i in range(1, vectors.nf):
            bias_block(vectors.at(i, 0))

    def vectors_second():
        for c in range(per):
            vectors.second(c)
        for j in range(1, vectors.ns):
            for i in range(vectors.nf):
                bias_block(vectors.at(i, j))

    def vectors_third():
        @pl.loop(1, nb // 2)
        def _(d):
            block = (vectors.sibling + 2 * d) % nb
            for c in range(per):
                vectors.landed(block, c)
            bias_block(block)

    for c in range(per):
        vectors.first(c)

    def first_term(c):
        for d in range(nb // 2):
            gather.landed((gather.sibling + 2 * d) % nb, c)
        terms[0, :, cols(c)] = jnp.dot(flat[...], field[:, cols(c)], preferred_element_type=f32).astype(bf16)

    @pl.loop(0, chunks + 6)
    def _(t):
        when_chunk(t, reduce_in)
        when_chunk(t - lag, spread)
        when_chunk(t - lag - 1, gather.first)
        when_chunk(t - lag - 2, gather.second)
        when_chunk(t - lag - 3, first_term)
        pl.when(t == lag)(vectors_first)
        pl.when(t == lag + 2)(vectors_second)
        pl.when(t == lag + 4)(vectors_third)

    biases = jnp.sum(acc[...], axis=1, keepdims=True)
    diagonal = lax.broadcasted_iota(jnp.int32, (group, group), 0) == lax.broadcasted_iota(jnp.int32, (group, group), 1)
    for w in range(wdev):
        column = jnp.broadcast_to(biases[w * group:(w + 1) * group], (group, group))
        fb[w:w + 1, :] = jnp.sum(jnp.where(diagonal, column, 0.0), axis=0, keepdims=True)

    tile = orbitals // 2
    for order in range(2, orders + 1):
        @pl.loop(0, orbitals // tile)
        def _(n):
            span = pl.ds(pl.multiple_of(n * tile, tile), tile)
            term = (jnp.dot(terms[order - 2], field[:, span], preferred_element_type=f32) / order).astype(bf16)
            if order == orders:
                value = flat[:, span].astype(f32)
                for k in range(orders - 1):
                    value = value + terms[k, :, span].astype(f32)
                out[:, span] = (value + term.astype(f32)).astype(bf16)
            else:
                terms[order - 1, :, span] = term

    vectors.drain()
    gather.drain()

    @pl.loop(0, chunks)
    def _(c):
        @pl.when(is_mid)
        def _():
            across(c).wait_send()

        @pl.when(jnp.logical_not(is_mid))
        def _():
            to_mid(c).wait_send()

        @pl.when(has_outer)
        def _():
            back(c).wait_send()


def local(nb, nw, walkers, inv_intersection, rotated_chol, full_chol, field_noise):
    wdev, double_rows, orbitals = walkers.shape
    occupied = double_rows // 2
    group = field_noise.shape[0]
    per = rotated_chol.shape[0]
    local_count, block_rows, _ = full_chol.shape
    chunks = 8
    size = orbitals // chunks
    split = orbitals // 2 // nw % 128 == 0
    half = orbitals // 2 if split else orbitals
    flat = walkers.reshape(wdev * double_rows, orbitals)
    inv = inv_intersection.transpose(0, 2, 1, 3).reshape(wdev, occupied, double_rows)
    vmem, hbm = pl.BlockSpec(memory_space=pltpu.VMEM), pl.BlockSpec(memory_space=pl.ANY)
    dma = pltpu.SemaphoreType.DMA
    out, fb, shift = pl.pallas_call(
        functools.partial(kernel, nb, nw, wdev * nb * nw, chunks, split),
        out_shape=(jax.ShapeDtypeStruct(flat.shape, bf16), jax.ShapeDtypeStruct((wdev, group), f32),
                   jax.ShapeDtypeStruct((1, group), f32)),
        in_specs=[vmem, vmem, vmem, hbm, hbm, vmem],
        out_specs=(vmem, vmem, vmem),
        scratch_shapes=[
            pltpu.VMEM((2, occupied, half), f32),
            pltpu.VMEM((occupied, half), f32),
            pltpu.VMEM((nw, occupied, half // nw), bf16),
            pltpu.VMEM((nw, occupied, half // nw), bf16),
            pltpu.VMEM((nb // 2 if split else nb, occupied, half // nw), bf16),
            pltpu.VMEM((group, occupied, orbitals), bf16),
            pltpu.VMEM(full_chol.shape, bf16),
            pltpu.VMEM((wdev, occupied, orbitals), bf16),
            pltpu.VMEM((wdev * group, orbitals), f32),
            pltpu.VMEM((orbitals, orbitals), bf16),
            pltpu.VMEM((chunks, block_rows, size), bf16),
            pltpu.VMEM((chunks, block_rows, size), bf16),
            pltpu.VMEM((chunks, block_rows, size), bf16),
            pltpu.VMEM((nw, 1, 128), f32),
            pltpu.VMEM((nb, 1, 128), f32),
            pltpu.VMEM((orders - 1,) + flat.shape, bf16),
            dma((nb, per)), dma, dma, dma,
            dma((nb, chunks)), dma, dma, dma,
            dma((2,)), dma((5,)), dma((5,)),
            dma((chunks,)), dma((chunks,)), dma((chunks,)), dma((chunks,)), dma((chunks,)), dma((chunks,)),
        ],
        compiler_params=pltpu.CompilerParams(collective_id=0, has_side_effects=True, vmem_limit_bytes=60 * 2**20),
    )(flat, walkers, inv, rotated_chol, full_chol, field_noise.reshape(1, group))
    return (out.reshape(walkers.shape), fb, shift.reshape(group))


def solution(mesh):
    placed = (
        P(("blk", "walk"), None, None),
        P(("blk", "walk"), None, None, None),
        P("blk", None, None),
        P("walk", "blk", None),
        P(),
    )
    return jax.shard_map(
        functools.partial(local, mesh.shape["blk"], mesh.shape["walk"]),
        mesh=mesh,
        in_specs=placed,
        out_specs=(P(("blk", "walk"), None, None), P(("blk", "walk"), None), P()),
        check_vma=False,
    )
```

```python
import functools
import math

import jax
import jax.numpy as jnp
from jax import lax
from jax.experimental import pallas as pl
from jax.experimental.pallas import tpu as pltpu
from jax.sharding import PartitionSpec as P

time_root = 0.1
orders = 4
f32, bf16 = jnp.float32, jnp.bfloat16


class Gather:
    def __init__(self, nb, chunks, ref_at, many, recv, send_f, send_s, send_b):
        self.nb, self.chunks, self.ref_at, self.many = nb, chunks, ref_at, many
        self.recv, self.send_f, self.send_s, self.send_b = recv, send_f, send_s, send_b
        me = lax.axis_index("blk")
        self.me, self.core = me, me % 2
        self.cols = 2 if nb % 4 == 0 else 1
        self.rows = nb // 2 // self.cols
        chip = me // 2
        col, row = chip % self.cols, chip // self.cols
        self.turn = self.core if self.rows == self.cols else 0
        self.f = (1 - self.turn) * col + self.turn * row
        self.s = (1 - self.turn) * row + self.turn * col
        self.nf, self.ns = self.cols, self.rows
        self.sibling = chip * 2 + 1 - self.core

    def at(self, i, j, core=None):
        f, s = (self.f + i) % self.nf, (self.s + j) % self.ns
        chip = (1 - self.turn) * (s * self.cols + f) + self.turn * (f * self.cols + s)
        return chip * 2 + (self.core if core is None else core)

    def copy(self, block, chunk, target, send):
        piece = self.ref_at(block, chunk)
        return pltpu.make_async_remote_copy(
            src_ref=piece, dst_ref=piece, send_sem=send, recv_sem=self.recv.at[block, chunk],
            device_id={"blk": target}, device_id_type=pl.DeviceIdType.MESH)

    def landed(self, block, chunk):
        self.copy(block, chunk, self.sibling, self.send_b).wait_recv()

    def own(self, chunk):
        self.far(chunk)
        self.near(chunk)

    def far(self, chunk):
        for i in range(1, self.nf):
            self.copy(self.me, chunk, self.at(i, 0), self.send_f).start()
        for j in range(1, self.ns):
            self.copy(self.me, chunk, self.at(0, j), self.send_s).start()

    def near(self, chunk):
        self.copy(self.me, chunk, self.sibling, self.send_b).start()

    def first(self, chunk):
        for i in range(1, self.nf):
            block = self.at(i, 0)
            self.landed(block, chunk)
            for j in range(1, self.ns):
                self.copy(block, chunk, self.at(0, j), self.send_s).start()
            self.copy(block, chunk, self.sibling, self.send_b).start()

    def second(self, chunk):
        for j in range(1, self.ns):
            for i in range(self.nf):
                block = self.at(i, j)
                self.landed(block, chunk)
                self.copy(block, chunk, self.sibling, self.send_b).start()

    def drain(self):
        for send, count in ((self.send_f, self.nf - 1), (self.send_s, (self.ns - 1) * self.nf), (self.send_b, self.nb // 2)):
            if count:
                piece = self.many(count)
                pltpu.make_async_remote_copy(
                    src_ref=piece, dst_ref=piece, send_sem=send, recv_sem=self.recv.at[0, 0],
                    device_id={"blk": self.sibling}, device_id_type=pl.DeviceIdType.MESH).wait_send()


def kernel(nb, nw, total_walkers, chunks, split, flat, three, inv, rot_hbm, full_hbm, noise,
           out, fb, shift,
           pair, mine, zout, zin, pin, rot, full, theta, acc, field, mid, outer_in, inner_in, slots_w, slots_b, terms,
           rot_recv, rot_f, rot_s, rot_b, fld_recv, fld_f, fld_s, fld_b,
           load, slot_send, slot_recv, in_send, in_recv, mid_send, mid_recv, out_send, out_recv):
    blk, walk = lax.axis_index("blk"), lax.axis_index("walk")
    wdev, occupied, orbitals = theta.shape
    per, group = rot_hbm.shape[0], rot.shape[0]
    local_count, block_rows = full_hbm.shape[0], full_hbm.shape[1]
    size = orbitals // chunks
    MESH = pl.DeviceIdType.MESH

    load_rot = pltpu.make_async_copy(rot_hbm, rot.at[pl.ds(blk * per, per)], load.at[0])
    load_rot.start()
    load_full = pltpu.make_async_copy(full_hbm, full, load.at[1])
    load_full.start()
    barrier = pltpu.get_barrier_semaphore()
    for d in range(1, nb):
        pl.semaphore_signal(barrier, inc=1, device_id={"blk": (blk + d) % nb}, device_id_type=MESH)
    for d in range(1, nw):
        pl.semaphore_signal(barrier, inc=1, device_id={"walk": (walk + d) % nw}, device_id_type=MESH)
    pl.semaphore_wait(barrier, nb + nw - 2)
    load_rot.wait()

    vectors = Gather(nb, per, lambda block, c: rot.at[block * per + c], lambda k: rot.at[pl.ds(0, k * per)],
                     rot_recv, rot_f, rot_s, rot_b)
    vectors.far(0)
    for c in range(per):
        vectors.near(c)

    def share(slots, source, me, peers, k):
        for peer, slot in peers:
            pltpu.make_async_remote_copy(
                src_ref=slots.at[me] if source is None else source.at[slot], dst_ref=slots.at[me],
                send_sem=slot_send.at[k], recv_sem=slot_recv.at[k], device_id=peer, device_id_type=MESH).start()

        def finish():
            rest = slots.at[pl.ds(0, len(peers))]
            pltpu.make_async_remote_copy(
                src_ref=rest, dst_ref=rest, send_sem=slot_send.at[k], recv_sem=slot_recv.at[k],
                device_id=peers[0][0], device_id_type=MESH).wait()

        return finish

    walk_peers = [({"walk": (walk + d) % nw}, (walk + d) % nw) for d in range(1, nw)]
    blk_peers = [({"blk": (blk + d) % nb}, (blk + d) % nb) for d in range(1, nb)]
    tile = 512
    parts, span_width = (2, pair.shape[-1]) if split else (1, orbitals)

    def project(begin, into):
        for lo in range(0, span_width, tile):
            span = pl.ds(pl.multiple_of(begin + lo, tile), tile)
            both = jnp.zeros((occupied, tile), f32)
            for w in range(wdev):
                one = jnp.dot(inv[w], three[w, :, span], preferred_element_type=f32).astype(bf16)
                theta[w, :, span] = one
                both = both + one.astype(f32)
            into[:, lo:lo + tile] = both

    first_column = 0
    if split:
        project((1 - vectors.core) * span_width, pair.at[0])
        swap = pltpu.make_async_remote_copy(
            src_ref=pair.at[0], dst_ref=pair.at[1], send_sem=slot_send.at[4], recv_sem=slot_recv.at[4],
            device_id={"blk": vectors.sibling}, device_id_type=MESH)
        swap.start()
        first_column = vectors.core * span_width
        project(first_column, mine)
        swap.wait()
    else:
        project(0, mine)
    width = span_width // nw
    for k in range(nw):
        value = mine[:, k * width:(k + 1) * width]
        if split:
            value = value + pair[1, :, k * width:(k + 1) * width]
        zout[k] = value.astype(bf16)
    zin[pl.ds(walk, 1)] = zout[pl.ds(walk, 1)]
    share(zin, zout, walk, walk_peers, 2)()
    value = zin[0].astype(f32)
    for k in range(1, nw):
        value = value + zin[k].astype(f32)
    if split:
        place = blk // 2
        plane_peers = [({"blk": (blk + 2 * d) % nb}, 0) for d in range(1, nb // 2)]
    else:
        place, plane_peers = blk, blk_peers
    pin[pl.ds(place, 1)] = value.astype(bf16)[None]
    finish = share(pin, None, place, plane_peers, 3)
    for c in range(1, per):
        vectors.far(c)
    for c in range(per):
        vectors.landed(vectors.sibling, c)
    finish()
    value = pin[0].astype(f32)
    for k in range(1, pin.shape[0]):
        value = value + pin[k].astype(f32)
    columns = pl.ds(pl.multiple_of(first_column + walk * width, width), width)
    spot = lax.broadcasted_iota(jnp.int32, (1, 128), 1)
    line = jnp.zeros((1, 128), f32)
    for c in range(per * parts):
        g = place * per * parts + c
        product = rot[g, :, columns].astype(f32) * value
        one = jnp.sum(jnp.sum(product, axis=0, keepdims=True), axis=1, keepdims=True)
        line = line + jnp.where(spot == g, one, 0.0)
    for peers, me, slots, k in ((walk_peers, walk, slots_w, 0), (blk_peers, blk, slots_b, 1)):
        slots[pl.ds(me, 1)] = line[None]
        share(slots, None, me, peers, k)()
        line = slots[0]
        for d in range(1, slots.shape[0]):
            line = line + slots[d]
    shifts = line / math.sqrt(total_walkers)
    shift[...] = shifts[:, 0:group]
    shifted = (noise[...] - shifts[:, 0:group]) * time_root
    lane = lax.broadcasted_iota(jnp.int32, (1, group), 1)
    weights = [jnp.sum(jnp.where(lane == walk * local_count + j, shifted, 0.0), axis=1, keepdims=True)
               for j in range(local_count)]
    load_full.wait()

    half = nw // 2
    low = walk < half
    is_mid = (walk == half - 1) | (walk == half)
    has_outer = (walk != 0) & (walk != nw - 1)
    step = 1 - 2 * (walk >= half).astype(jnp.int32)
    inward = (walk + step + nw) % nw
    outward = (walk - step + nw) % nw
    lag = jnp.where(is_mid, 1, 4)
    cols = lambda c: pl.ds(pl.multiple_of(c * size, size), size)
    rows = lambda block: pl.ds(pl.multiple_of(block * block_rows, block_rows), block_rows)
    part_at = lambda block, c: field.at[rows(block), cols(c)]
    gather = Gather(nb, chunks, part_at, lambda k: field.at[pl.ds(0, k * block_rows)], fld_recv, fld_f, fld_s, fld_b)

    def hop(src, dst, send, recv, target):
        return pltpu.make_async_remote_copy(src_ref=src, dst_ref=dst, send_sem=send, recv_sem=recv,
                                            device_id={"walk": target}, device_id_type=MESH)

    def to_mid(c):
        return hop(mid.at[c], outer_in.at[c], in_send.at[c], in_recv.at[c], inward)

    def across(c):
        return hop(mid.at[c], inner_in.at[c], mid_send.at[c], mid_recv.at[c], inward)

    def back(c):
        return hop(part_at(blk, c), part_at(blk, c), out_send.at[c], out_recv.at[c], outward)

    def reduce_in(c):
        def summed():
            value = weights[0] * full[0, :, cols(c)].astype(f32)
            for j in range(1, local_count):
                value = value + weights[j] * full[j, :, cols(c)].astype(f32)
            return value

        @pl.when(has_outer)
        def _():
            to_mid(c).wait_recv()
            mid[c] = (summed() + outer_in[c].astype(f32)).astype(bf16)

        @pl.when(jnp.logical_not(has_outer))
        def _():
            mid[c] = summed().astype(bf16)

        @pl.when(is_mid)
        def _():
            across(c).start()

        @pl.when(jnp.logical_not(is_mid))
        def _():
            to_mid(c).start()

    def spread(c):
        @pl.when(is_mid)
        def _():
            across(c).wait_recv()
            field[rows(blk), cols(c)] = (mid[c].astype(f32) + inner_in[c].astype(f32)).astype(bf16)

        @pl.when(jnp.logical_not(is_mid))
        def _():
            back(c).wait_recv()

        @pl.when(has_outer)
        def _():
            back(c).start()

        gather.own(c)

    def when_chunk(c, action):
        @pl.when((c >= 0) & (c < chunks))
        def _():
            action(c)

    def bias(g):
        for lo in range(0, orbitals, 256):
            vector = rot[g, :, lo:lo + 256].astype(f32)
            for w in range(wdev):
                product = vector * theta[w, :, lo:lo + 256].astype(f32)
                acc[pl.ds(w * group + g, 1), lo:lo + 256] = jnp.sum(product, axis=0, keepdims=True)

    def bias_block(block):
        @pl.loop(0, per)
        def _(c):
            bias(block * per + c)

    def vectors_first():
        bias_block(blk)
        bias_block(vectors.sibling)
        for i in range(1, vectors.nf):
            bias_block(vectors.at(i, 0))

    def vectors_second():
        for c in range(per):
            vectors.second(c)
        for j in range(1, vectors.ns):
            for i in range(vectors.nf):
                bias_block(vectors.at(i, j))

    def vectors_third():
        @pl.loop(1, nb // 2)
        def _(d):
            block = (vectors.sibling + 2 * d) % nb
            for c in range(per):
                vectors.landed(block, c)
            bias_block(block)

    for c in range(per):
        vectors.first(c)

    def first_term(c):
        for d in range(nb // 2):
            gather.landed((gather.sibling + 2 * d) % nb, c)
        terms[0, :, cols(c)] = jnp.dot(flat[...], field[:, cols(c)], preferred_element_type=f32).astype(bf16)

    @pl.loop(0, chunks + 7)
    def _(t):
        when_chunk(t, reduce_in)
        when_chunk(t - lag, spread)
        when_chunk(t - lag - 1, gather.first)
        when_chunk(t - lag - 2, gather.second)
        when_chunk(t - lag - 3, first_term)
        pl.when(t == lag)(vectors_first)
        pl.when(t == lag + 2)(vectors_second)
        pl.when(t == lag + 4)(vectors_third)

    biases = jnp.sum(acc[...], axis=1, keepdims=True)
    diagonal = lax.broadcasted_iota(jnp.int32, (group, group), 0) == lax.broadcasted_iota(jnp.int32, (group, group), 1)
    for w in range(wdev):
        column = jnp.broadcast_to(biases[w * group:(w + 1) * group], (group, group))
        fb[w:w + 1, :] = jnp.sum(jnp.where(diagonal, column, 0.0), axis=0, keepdims=True)

    tile = orbitals // 2
    for order in range(2, orders + 1):
        @pl.loop(0, orbitals // tile)
        def _(n):
            span = pl.ds(pl.multiple_of(n * tile, tile), tile)
            term = (jnp.dot(terms[order - 2], field[:, span], preferred_element_type=f32) / order).astype(bf16)
            if order == orders:
                value = flat[:, span].astype(f32)
                for k in range(orders - 1):
                    value = value + terms[k, :, span].astype(f32)
                out[:, span] = (value + term.astype(f32)).astype(bf16)
            else:
                terms[order - 1, :, span] = term

    vectors.drain()
    gather.drain()

    @pl.loop(0, chunks)
    def _(c):
        @pl.when(is_mid)
        def _():
            across(c).wait_send()

        @pl.when(jnp.logical_not(is_mid))
        def _():
            to_mid(c).wait_send()

        @pl.when(has_outer)
        def _():
            back(c).wait_send()


def local(nb, nw, walkers, inv_intersection, rotated_chol, full_chol, field_noise):
    wdev, double_rows, orbitals = walkers.shape
    occupied = double_rows // 2
    group = field_noise.shape[0]
    per = rotated_chol.shape[0]
    local_count, block_rows, _ = full_chol.shape
    chunks = 8
    size = orbitals // chunks
    split = orbitals // 2 // nw % 128 == 0
    half = orbitals // 2 if split else orbitals
    flat = walkers.reshape(wdev * double_rows, orbitals)
    inv = inv_intersection.transpose(0, 2, 1, 3).reshape(wdev, occupied, double_rows)
    vmem, hbm = pl.BlockSpec(memory_space=pltpu.VMEM), pl.BlockSpec(memory_space=pl.ANY)
    dma = pltpu.SemaphoreType.DMA
    out, fb, shift = pl.pallas_call(
        functools.partial(kernel, nb, nw, wdev * nb * nw, chunks, split),
        out_shape=(jax.ShapeDtypeStruct(flat.shape, bf16), jax.ShapeDtypeStruct((wdev, group), f32),
                   jax.ShapeDtypeStruct((1, group), f32)),
        in_specs=[vmem, vmem, vmem, hbm, hbm, vmem],
        out_specs=(vmem, vmem, vmem),
        scratch_shapes=[
            pltpu.VMEM((2, occupied, half), f32),
            pltpu.VMEM((occupied, half), f32),
            pltpu.VMEM((nw, occupied, half // nw), bf16),
            pltpu.VMEM((nw, occupied, half // nw), bf16),
            pltpu.VMEM((nb // 2 if split else nb, occupied, half // nw), bf16),
            pltpu.VMEM((group, occupied, orbitals), bf16),
            pltpu.VMEM(full_chol.shape, bf16),
            pltpu.VMEM((wdev, occupied, orbitals), bf16),
            pltpu.VMEM((wdev * group, orbitals), f32),
            pltpu.VMEM((orbitals, orbitals), bf16),
            pltpu.VMEM((chunks, block_rows, size), bf16),
            pltpu.VMEM((chunks, block_rows, size), bf16),
            pltpu.VMEM((chunks, block_rows, size), bf16),
            pltpu.VMEM((nw, 1, 128), f32),
            pltpu.VMEM((nb, 1, 128), f32),
            pltpu.VMEM((orders - 1,) + flat.shape, bf16),
            dma((nb, per)), dma, dma, dma,
            dma((nb, chunks)), dma, dma, dma,
            dma((2,)), dma((5,)), dma((5,)),
            dma((chunks,)), dma((chunks,)), dma((chunks,)), dma((chunks,)), dma((chunks,)), dma((chunks,)),
        ],
        compiler_params=pltpu.CompilerParams(collective_id=0, has_side_effects=True, vmem_limit_bytes=60 * 2**20),
    )(flat, walkers, inv, rotated_chol, full_chol, field_noise.reshape(1, group))
    return (out.reshape(walkers.shape), fb, shift.reshape(group))


def solution(mesh):
    placed = (
        P(("blk", "walk"), None, None),
        P(("blk", "walk"), None, None, None),
        P("blk", None, None),
        P("walk", "blk", None),
        P(),
    )
    return jax.shard_map(
        functools.partial(local, mesh.shape["blk"], mesh.shape["walk"]),
        mesh=mesh,
        in_specs=placed,
        out_specs=(P(("blk", "walk"), None, None), P(("blk", "walk"), None), P()),
        check_vma=False,
    )
```
